32 devices in a mesh: dp: 8 (over z, y), tp: 4 (over x, core).
Axes of the slice: x: 2, y: 2, z: 4, core: 2. Of those that a mesh axis runs over, the one named last changes fastest.
Arguments:
- tokens: bfloat16 [32, 256, 2048], P('dp'), may hold values from -6 to 6
- cotangent: bfloat16 [32, 256, 2048], P('dp'), may hold values from -6 to 6
- lengths: int32 [32], P('dp'), may hold values from 192 to 256, as said below
- action_counts: int32 [32, 8], P('dp'), may hold values from 1 to 8
- qkv_weight: bfloat16 [2048, 3, 2048], P('dp', None, 'tp'), may hold values from -0.125 to 0.125
- out_weight: bfloat16 [2048, 2048], P('dp', 'tp'), may hold values from -0.5 to 0.5
- up_weight: bfloat16 [2048, 8192], P('dp', 'tp'), may hold values from -0.125 to 0.125
- down_weight: bfloat16 [2048, 8192], P('dp', 'tp'), may hold values from -0.0625 to 0.0625
- gain_one: bfloat16 [2048], P('dp'), may hold values from 0.099609375 to 1.8984375
- shift_one: bfloat16 [2048], P('dp'), may hold values from -3 to 3
- gain_two: bfloat16 [2048], P('dp'), may hold values from 0.099609375 to 1.8984375
- shift_two: bfloat16 [2048], P('dp'), may hold values from -3 to 3
Outputs:
- layer_out: bfloat16 [32, 256, 2048], P('dp')
- input_grad: float32 [32, 256, 2048], P('dp')
- qkv_grad: float32 [2048, 3, 2048], P('dp', None, 'tp')
- out_grad: float32 [2048, 2048], P('dp', 'tp')
- up_grad: float32 [2048, 8192], P('dp', 'tp')
- down_grad: float32 [2048, 8192], P('dp', 'tp')
- gain_one_grad: float32 [2048], P('dp')
- shift_one_grad: float32 [2048], P('dp')
- gain_two_grad: float32 [2048], P('dp')
- shift_two_grad: float32 [2048], P('dp')
The draws below stay inside these ranges and needn't reach their ends.
Inputs may be any that keep to these rules, and one draw needn't show every extreme that they name: `lengths`: every item has at least 192 valid slots; some item has exactly that many and some item is full.
All inputs are finite; a program needn't handle non-finite values.
Results may differ from the reference program's by a relative error of at most 0.023.
Values may be sent and summed in bfloat16 or wider, within the bound.
No kernel may reach another device: no remote copies, remote signals or barrier semaphores. Data moves between devices by JAX's collectives and lax.ppermute only.
A program may use at most 256 MiB of HBM per device.

```python
import jax
import jax.numpy as jnp
from jax import lax

D = 2048
HEADS = 16
HEAD_DIM = 128
FF = 8192
SLOTS = 256
STEP_SLOTS = 32
ACTIONS = 8
ITEMS = 32
STEPS = 8
N_DP = 8


def draw_lengths(key, part):
    first_key, second_key = jax.random.split(key)
    values = jax.random.randint(first_key, (ITEMS,), SLOTS * 3 // 4, SLOTS + 1)
    chosen = jax.random.randint(second_key, (), 0, ITEMS)
    index = jnp.arange(ITEMS, dtype=jnp.int32)
    values = jnp.where(index == chosen, SLOTS, values)
    values = jnp.where(index == (chosen + 1) % ITEMS, SLOTS * 3 // 4, values)
    return values.astype(jnp.int32)


def plant(values, own_key, smallest, high):
    index_at = [jax.random.randint(jax.random.fold_in(own_key, axis), (), 0, length) for axis, length in enumerate(values.shape)]
    widest = values.shape.index(max(values.shape))
    neighbour = index_at[:widest] + [(index_at[widest] + 1) % values.shape[widest]] + index_at[widest + 1:]
    return values.at[tuple(index_at)].set(smallest).at[tuple(neighbour)].set(high)


def levels(rng, dims, cuts, least, high):
    def one(axis_at, parts):
        heights = jax.random.uniform(jax.random.fold_in(jax.random.fold_in(rng, 6), axis_at), (parts,), jnp.float32, least / len(cuts), high / len(cuts))
        return jnp.repeat(jnp.exp(heights), dims[axis_at] // parts).reshape((-1,) + (1,) * (len(dims) - axis_at - 1))

    level = one(*cuts[0])
    for cut in cuts[1:]:
        level = level * one(*cut)
    return level


def bell_draw(key, shape, scale, reach, pieces=(), kind=jnp.bfloat16):
    factor_of = levels(key, shape, pieces, -0.22, 0.18) if pieces else 1.0
    drawn = jax.random.normal(key, shape, jnp.float32) * scale * factor_of
    return jnp.minimum(jnp.maximum(drawn, -reach), reach).astype(kind)


def setup_inputs(seed: int = 0) -> dict:
    arg_keys = jax.random.split(jax.random.key(seed), 13)
    tokens = bell_draw(arg_keys[0], (ITEMS, SLOTS, D), 1.0, 6.0, ((0, 8),))
    cotangent = bell_draw(arg_keys[1], (ITEMS, SLOTS, D), 1.0, 6.0, ((0, 8),))
    lengths = draw_lengths(jax.random.fold_in(arg_keys[12], 71), 0)
    action_counts = plant(jax.random.randint(arg_keys[3], (ITEMS, STEPS), 1, ACTIONS + 1), jax.random.fold_in(arg_keys[3], 1), 1, ACTIONS).astype(jnp.int32)
    qkv_weight = bell_draw(arg_keys[4], (D, 3, HEADS * HEAD_DIM), D ** -0.5, 0.125, ((0, 8), (2, 4)))
    out_weight = bell_draw(arg_keys[5], (D, HEADS * HEAD_DIM), (D // 16) ** -0.5, 0.5, ((0, 8), (1, 4)))
    up_weight = bell_draw(arg_keys[6], (D, FF), D ** -0.5, 0.125, ((0, 8), (1, 4)))
    down_weight = bell_draw(arg_keys[7], (D, FF), FF ** -0.5, 0.0625, ((0, 8), (1, 4)))
    gain_one = jnp.clip(1.0 + 0.18 * jax.random.normal(arg_keys[8], (D,), jnp.float32), 0.099609375, 1.8984375).astype(jnp.bfloat16)
    shift_one = bell_draw(arg_keys[9], (D,), 0.5, 3.0, ((0, 8),))
    gain_two = jnp.clip(1.0 + 0.18 * jax.random.normal(arg_keys[10], (D,), jnp.float32), 0.099609375, 1.8984375).astype(jnp.bfloat16)
    shift_two = bell_draw(arg_keys[11], (D,), 0.5, 3.0, ((0, 8),))
    return dict(tokens=tokens, cotangent=cotangent, lengths=lengths, action_counts=action_counts, qkv_weight=qkv_weight, out_weight=out_weight, up_weight=up_weight, down_weight=down_weight, gain_one=gain_one, shift_one=shift_one, gain_two=gain_two, shift_two=shift_two)


highest = lax.Precision.HIGHEST
norm_epsilon = 1e-05
masked_score = -1e+30

@jax.custom_vjp
def low(v):
    return lax.optimization_barrier(v.astype(jnp.bfloat16)).astype(jnp.float32)

@jax.custom_vjp
def low_back(v):
    return v

def low_keep(v):
    return (low(v), None)

def low_pass(kept, grad):
    return (grad,)

def back_keep(v):
    return (v, None)

def back_low(kept, grad):
    return (low(grad),)
low.defvjp(low_keep, low_pass)
low_back.defvjp(back_keep, back_low)

def layer_norm(values, gain, shift):
    center = lax.optimization_barrier(jnp.mean(values, axis=-1, keepdims=True))
    offset = values - center
    spread = lax.optimization_barrier(jnp.mean(offset * offset, axis=-1, keepdims=True))
    return offset * lax.rsqrt(spread + norm_epsilon) * gain + shift

def gelu_exact(values):
    return jax.nn.gelu(values, approximate=False)

def row_weights(item_lengths, item_actions, slot_count):
    position = jnp.arange(slot_count, dtype=jnp.int32)
    in_step = position % STEP_SLOTS
    counts = jnp.repeat(item_actions, STEP_SLOTS, axis=1)
    is_valid = position[None, :] < item_lengths[:, None]
    is_action = in_step[None, :] >= STEP_SLOTS - counts
    return jnp.where(is_valid, jnp.where(is_action, 1.0, 0.5), 0.0).astype(jnp.float32)

def attend_item(inputs):
    queries, key_heads, value_heads, length = inputs
    position = jnp.arange(SLOTS, dtype=jnp.int32)
    allowed = (position[None, :] <= position[:, None]) & (position[None, :] < length)
    scores = jnp.einsum('qhd,khd->hqk', queries, key_heads, precision=highest) * HEAD_DIM ** (-0.5)
    scores = low_back(scores)
    scores = jnp.where(allowed[None], scores, masked_score)
    row_max = lax.optimization_barrier(jnp.max(scores, axis=-1, keepdims=True))
    exponent = jnp.exp(scores - row_max)
    attention_probs = low(exponent / lax.optimization_barrier(jnp.sum(exponent, axis=-1, keepdims=True)))
    return jnp.einsum('hqk,khd->qhd', attention_probs, value_heads, precision=highest)

def layer_block(tokens_f, qkv_w, out_w, up_w, down_w, gain_one, shift_one, gain_two, shift_two, item_lengths):
    group_size, slot_count, model_width = tokens_f.shape
    normed_one = low(layer_norm(tokens_f, gain_one, shift_one))
    projected = low(low_back(jnp.einsum('gsd,dch->gsch', normed_one, qkv_w, precision=highest)))
    head_shape = (group_size, slot_count, HEADS, HEAD_DIM)
    attended = lax.map(jax.checkpoint(attend_item), (projected[:, :, 0].reshape(head_shape), projected[:, :, 1].reshape(head_shape), projected[:, :, 2].reshape(head_shape), item_lengths))
    attended = low(low_back(attended.reshape(group_size, slot_count, HEADS * HEAD_DIM)))
    branch = low_back(jnp.einsum('gsh,dh->gsd', attended, out_w, precision=highest))
    middle = tokens_f + branch
    normed_two = low(layer_norm(middle, gain_two, shift_two))
    up_proj = low_back(jnp.einsum('gsd,df->gsf', normed_two, up_w, precision=highest))
    activated = low(gelu_exact(up_proj))
    down_proj = low_back(jnp.einsum('gsf,df->gsd', activated, down_w, precision=highest))
    return middle + down_proj

def reference(tokens, cotangent, lengths, action_counts, qkv_weight, out_weight, up_weight, down_weight, gain_one, shift_one, gain_two, shift_two):
    params = tuple((weight_in.astype(jnp.float32) for weight_in in (qkv_weight, out_weight, up_weight, down_weight, gain_one, shift_one, gain_two, shift_two)))
    group_size = ITEMS // N_DP
    group_shape = (N_DP, group_size, SLOTS, D)

    def one_group(totals, inputs):
        tokens_group, cot_group, lengths_group, actions_group = inputs

        def forward(tokens_f, *weights):
            return layer_block(tokens_f, *weights, lengths_group)
        result, pullback = jax.vjp(forward, tokens_group.astype(jnp.float32), *params)
        weighted_cot = cot_group.astype(jnp.float32) * row_weights(lengths_group, actions_group, SLOTS)[:, :, None]
        gradients = pullback(weighted_cot)
        totals = tuple((total + extra for total, extra in zip(totals, gradients[1:])))
        return (totals, (result.astype(jnp.bfloat16), gradients[0]))
    initial = tuple((jnp.zeros(weight_in.shape, jnp.float32) for weight_in in params))
    totals, (outputs, input_grad) = lax.scan(one_group, initial, (tokens.reshape(group_shape), cotangent.reshape(group_shape), lengths.reshape(N_DP, group_size), action_counts.reshape(N_DP, group_size, STEPS)))
    return (outputs.reshape(ITEMS, SLOTS, D), input_grad.reshape(ITEMS, SLOTS, D), totals[0], totals[1], totals[2], totals[3], totals[4], totals[5], totals[6], totals[7])
```

```python
import jax
import jax.numpy as jnp
from jax import lax
from jax.sharding import PartitionSpec as P

HEAD_DIM = 128
STEP_SLOTS = 32


norm_epsilon = 1e-05
masked_score = -1e30
f32 = jnp.float32
bf16 = jnp.bfloat16


def dot(subscripts, a, b):
    return jnp.einsum(subscripts, a, b, preferred_element_type=f32)


class Places:
    def __init__(self):
        self.dp = lax.axis_size("dp")
        self.tp = lax.axis_size("tp")
        self.ring_size = self.dp // 2
        index = lax.axis_index("dp")
        self.ring_at = index // 2
        self.pair_at = index % 2
        self.dp_at = index
        self.core = lax.axis_index("tp") % 2

    def ring(self, value):
        return lax.ppermute(value, "dp", [(i, (i + 2) % self.dp) for i in range(self.dp)])

    def pair(self, value):
        return lax.ppermute(value, "dp", [(i, i ^ 1) for i in range(self.dp)])

    def shift(self, value, by):
        return lax.ppermute(value, "dp", [(i, (i + by) % self.dp) for i in range(self.dp)])

    def other_core(self, value):
        return lax.ppermute(value, "tp", [(i, i ^ 1) for i in range(self.tp)])

    def chips_sum(self, value):
        chips = self.tp // 2
        total = value.astype(f32)
        for by in range(1, chips):
            moved = lax.ppermute(
                value, "tp", [(i, (i + 2 * by) % self.tp) for i in range(self.tp)]
            )
            total = total + moved.astype(f32)
        return total


def gather(at, shard):
    full = jnp.zeros((at.dp,) + shard.shape, shard.dtype)
    piece = shard
    for step in range(at.ring_size):
        owner = (at.ring_at - step) % at.ring_size
        start = (0,) * shard.ndim
        full = lax.dynamic_update_slice(full, piece[None], (2 * owner + at.pair_at,) + start)
        full = lax.dynamic_update_slice(
            full, at.pair(piece)[None], (2 * owner + 1 - at.pair_at,) + start
        )
        if step + 1 < at.ring_size:
            piece = at.ring(piece)
    return full.reshape((at.dp * shard.shape[0],) + shard.shape[1:])


def weight_grad(at, left, right):
    width = left.shape[1] // at.dp

    def part(block):
        columns = lax.dynamic_slice_in_dim(left, block * width, width, axis=1)
        return dot("rd,rf->df", columns, right)

    carried = None
    for step in range(at.ring_size):
        owner = (at.ring_at - 1 - step) % at.ring_size
        for_pair = part(2 * owner + 1 - at.pair_at).astype(bf16)
        total = part(2 * owner + at.pair_at) + at.pair(for_pair).astype(f32)
        if carried is not None:
            total = total + carried.astype(f32)
        if step + 1 < at.ring_size:
            carried = at.ring(total.astype(bf16))
    return total


def half_of(at, value, which):
    size = value.shape[0] // 2
    return lax.dynamic_slice_in_dim(value, which * size, size, axis=0)


def summed_half(at, partial):
    for_other = half_of(at, partial, 1 - at.core)
    mine = half_of(at, partial, at.core).astype(f32)
    chip = mine + at.other_core(for_other).astype(f32)
    return at.chips_sum(chip.astype(bf16))


def both_halves(at, half):
    other = at.other_core(half)
    first = jnp.where(at.core == 0, half, other)
    second = jnp.where(at.core == 0, other, half)
    return jnp.concatenate([first, second], axis=0)


def normalize(values):
    center = jnp.mean(values, axis=-1, keepdims=True)
    offset = values - center
    spread = jnp.mean(offset * offset, axis=-1, keepdims=True)
    scale = lax.rsqrt(spread + norm_epsilon)
    return offset * scale, scale


def norm_back(grad, normal, scale, gain):
    gain_grad = jnp.sum(grad * normal, axis=0)
    shift_grad = jnp.sum(grad, axis=0)
    e = grad * gain
    mean_e = jnp.mean(e, axis=-1, keepdims=True)
    mean_en = jnp.mean(e * normal, axis=-1, keepdims=True)
    return scale * (e - mean_e - normal * mean_en), gain_grad, shift_grad


def gelu_exact(values):
    return jax.nn.gelu(values, approximate=False)


def row_weights(item_lengths, item_actions, slot_count):
    position = jnp.arange(slot_count, dtype=jnp.int32)
    in_step = position % STEP_SLOTS
    counts = jnp.repeat(item_actions, STEP_SLOTS, axis=1)
    is_valid = position[None, :] < item_lengths[:, None]
    is_action = in_step[None, :] >= STEP_SLOTS - counts
    return jnp.where(is_valid, jnp.where(is_action, 1.0, 0.5), 0.0).astype(f32)


def causal_allowed(item_lengths, slot_count):
    position = jnp.arange(slot_count, dtype=jnp.int32)
    return (position[None, None, :] <= position[None, :, None]) & (
        position[None, None, :] < item_lengths[:, None, None]
    )


def masked_scores(queries, key_heads, allowed):
    scores = dot("cqhd,ckhd->chqk", queries, key_heads) * HEAD_DIM ** (-0.5)
    return jnp.where(allowed[:, None], scores, masked_score)


def body(
    tokens,
    cotangent,
    lengths,
    action_counts,
    qkv_weight,
    out_weight,
    up_weight,
    down_weight,
    gain_one,
    shift_one,
    gain_two,
    shift_two,
):
    at = Places()
    item_count, slot_count, width = tokens.shape
    rows = item_count * slot_count
    shard_rows, kinds, head_width = qkv_weight.shape

    norm_params = gather(at, jnp.stack([gain_one, shift_one, gain_two, shift_two])[None])
    norm_params = norm_params.transpose(1, 0, 2).reshape(4, width).astype(f32)
    gain_1, shift_1, gain_2, shift_2 = norm_params
    qkv_w = gather(at, qkv_weight.reshape(shard_rows, kinds * head_width))
    out_w = gather(at, out_weight)
    up_w = gather(at, up_weight)
    down_w = gather(at, down_weight)

    tokens_f = tokens.astype(f32).reshape(rows, width)
    weighting = row_weights(lengths, action_counts, slot_count).reshape(rows, 1)
    grad_out = cotangent.astype(f32).reshape(rows, width) * weighting
    grad_low = grad_out.astype(bf16)

    normal_1, _ = normalize(tokens_f)
    normed_one = (normal_1 * gain_1 + shift_1).astype(bf16)
    projected = dot("rd,df->rf", normed_one, qkv_w).astype(bf16)
    projected = projected.reshape(rows, kinds, head_width)
    head_shape = (item_count, slot_count, head_width // HEAD_DIM, HEAD_DIM)
    queries = projected[:, 0].reshape(head_shape)
    key_heads = projected[:, 1].reshape(head_shape)
    value_heads = projected[:, 2].reshape(head_shape)
    allowed = causal_allowed(lengths, slot_count)
    scores = masked_scores(queries, key_heads, allowed)
    row_max = jnp.max(scores, axis=-1, keepdims=True)
    exponent = jnp.exp(scores - row_max)
    row_total = jnp.sum(exponent, axis=-1, keepdims=True)
    log_total = row_max + jnp.log(row_total)
    probs_low = (exponent / row_total).astype(bf16)
    attended = dot("chqk,ckhd->cqhd", probs_low, value_heads).astype(bf16)
    attended = attended.reshape(rows, head_width)

    branch = summed_half(at, dot("rh,dh->rd", attended, out_w).astype(bf16))
    tokens_half = half_of(at, tokens_f, at.core)
    middle = tokens_half + branch
    normal_2, scale_2 = normalize(middle)
    normed_two = both_halves(at, (normal_2 * gain_2 + shift_2).astype(bf16))

    up_proj = dot("rd,df->rf", normed_two, up_w)
    activated, gelu_back = jax.vjp(gelu_exact, up_proj)
    activated = activated.astype(bf16)
    down_grad = weight_grad(at, grad_low, activated)
    grad_act = dot("rd,df->rf", grad_low, down_w)
    (grad_up,) = gelu_back(grad_act)
    grad_up = grad_up.astype(bf16)

    grad_normed_two = summed_half(at, dot("rf,df->rd", grad_up, up_w).astype(bf16))
    down_proj = summed_half(at, dot("rf,df->rd", activated, down_w).astype(bf16))
    layer_out = both_halves(at, (middle + down_proj).astype(bf16))
    up_grad = weight_grad(at, normed_two, grad_up)

    grad_middle, gain_two_grad, shift_two_grad = norm_back(
        grad_normed_two, normal_2, scale_2, gain_2
    )
    grad_middle = grad_middle + half_of(at, grad_out, at.core)
    grad_branch = both_halves(at, grad_middle.astype(bf16))
    out_grad = weight_grad(at, grad_branch, attended)
    grad_attended = dot("rd,dh->rh", grad_branch, out_w).astype(bf16).reshape(head_shape)

    exact_probs = jnp.exp(masked_scores(queries, key_heads, allowed) - log_total)
    grad_value = dot("chqk,cqhd->ckhd", exact_probs.astype(bf16), grad_attended).astype(bf16)
    grad_probs = dot("cqhd,ckhd->chqk", grad_attended, value_heads)
    inner = jnp.sum(exact_probs * grad_probs, axis=-1, keepdims=True)
    grad_scores = (exact_probs * (grad_probs - inner)).astype(bf16)
    scaling = HEAD_DIM ** (-0.5)
    grad_query = (dot("chqk,ckhd->cqhd", grad_scores, key_heads) * scaling).astype(bf16)
    grad_key = (dot("chqk,cqhd->ckhd", grad_scores, queries) * scaling).astype(bf16)
    grad_projected = jnp.concatenate(
        [part.reshape(rows, head_width) for part in (grad_query, grad_key, grad_value)], axis=1
    )

    grad_normed_one = summed_half(at, dot("rf,df->rd", grad_projected, qkv_w).astype(bf16))
    qkv_grad = weight_grad(at, normed_one, grad_projected)
    normal_half, scale_half = normalize(tokens_half)
    grad_tokens, gain_one_grad, shift_one_grad = norm_back(
        grad_normed_one, normal_half, scale_half, gain_1
    )
    input_grad = both_halves(at, grad_tokens + grad_middle)

    norm_grads = jnp.stack([gain_one_grad, shift_one_grad, gain_two_grad, shift_two_grad])
    norm_grads = norm_grads + at.other_core(norm_grads)
    blocks = norm_grads.reshape(4, at.dp, shard_rows).transpose(1, 0, 2)
    norm_total = lax.dynamic_index_in_dim(blocks, at.dp_at, axis=0, keepdims=False)
    for by in range(1, at.dp):
        block = lax.dynamic_index_in_dim(
            blocks, (at.dp_at + by) % at.dp, axis=0, keepdims=False
        )
        norm_total = norm_total + at.shift(block, by)

    return (
        layer_out.reshape(tokens.shape),
        input_grad.reshape(tokens.shape),
        qkv_grad.reshape(qkv_weight.shape),
        out_grad,
        up_grad,
        down_grad,
        norm_total[0],
        norm_total[1],
        norm_total[2],
        norm_total[3],
    )


def solution(mesh):
    weight = P("dp", "tp")
    return jax.shard_map(
        body,
        mesh=mesh,
        in_specs=(
            P("dp", None, None),
            P("dp", None, None),
            P("dp"),
            P("dp", None),
            P("dp", None, "tp"),
            weight,
            weight,
            weight,
            P("dp"),
            P("dp"),
            P("dp"),
            P("dp"),
        ),
        out_specs=(
            P("dp", None, None),
            P("dp", None, None),
            P("dp", None, "tp"),
            weight,
            weight,
            weight,
            P("dp"),
            P("dp"),
            P("dp"),
            P("dp"),
        ),
        check_vma=False,
    )
```

```python
import jax
import jax.numpy as jnp
from jax import lax
from jax.sharding import PartitionSpec as P


HEAD_DIM = 128
STEP_SLOTS = 32


norm_epsilon = 1e-05
masked_score = -1e30
f32 = jnp.float32
bf16 = jnp.bfloat16


def dot(subscripts, a, b):
    return jnp.einsum(subscripts, a, b, preferred_element_type=f32)


class Places:
    def __init__(self):
        self.dp = lax.axis_size("dp")
        self.tp = lax.axis_size("tp")
        self.ring_size = self.dp // 2
        index = lax.axis_index("dp")
        self.ring_at = index // 2
        self.pair_at = index % 2
        self.dp_at = index
        self.core = lax.axis_index("tp") % 2

    def ring(self, value):
        return lax.ppermute(value, "dp", [(i, (i + 2) % self.dp) for i in range(self.dp)])

    def pair(self, value):
        return lax.ppermute(value, "dp", [(i, i ^ 1) for i in range(self.dp)])

    def shift(self, value, by):
        return lax.ppermute(value, "dp", [(i, (i + by) % self.dp) for i in range(self.dp)])

    def other_core(self, value):
        return lax.ppermute(value, "tp", [(i, i ^ 1) for i in range(self.tp)])

    def chips_sum(self, value):
        chips = self.tp // 2
        total = value.astype(f32)
        for by in range(1, chips):
            moved = lax.ppermute(
                value, "tp", [(i, (i + 2 * by) % self.tp) for i in range(self.tp)]
            )
            total = total + moved.astype(f32)
        return total


def cuts(columns):
    unit = 128
    on_b = columns // (6 * unit) * unit
    on_a = columns - on_b
    if on_b == 0:
        return [(0, columns, "A")]
    first = -(-on_a // (2 * unit)) * unit
    return [(0, first, "A"), (first, on_a - first, "A"), (on_a, on_b, "B")]


def gather(at, shard):
    rows, columns = shard.shape
    full = jnp.zeros((at.dp, rows, columns), shard.dtype)

    def put(full, piece, block, first):
        return lax.dynamic_update_slice(full, piece[None], (block, 0, first))

    for first, size, route in cuts(columns):
        piece = shard[:, first : first + size]
        if route == "B":
            piece = jnp.stack([piece, at.pair(piece)])
        for step in range(at.ring_size):
            owner = (at.ring_at - step) % at.ring_size
            own_block, pair_block = 2 * owner + at.pair_at, 2 * owner + 1 - at.pair_at
            if route == "A":
                full = put(full, piece, own_block, first)
                moved = at.pair(piece)
                full = put(full, moved, pair_block, first)
            else:
                full = put(full, piece[0], own_block, first)
                full = put(full, piece[1], pair_block, first)
            if step + 1 < at.ring_size:
                piece = at.ring(piece)
    return full.reshape(at.dp * rows, columns)


def weight_grad(at, left, right):
    width = left.shape[1] // at.dp

    def part(block, right):
        columns = lax.dynamic_slice_in_dim(left, block * width, width, axis=1)
        return dot("rd,rf->df", columns, right)

    totals = []
    for first, size, route in cuts(right.shape[1]):
        piece = right[:, first : first + size]
        carried = None
        for step in range(at.ring_size):
            owner = (at.ring_at - 1 - step) % at.ring_size
            own_block, pair_block = 2 * owner + at.pair_at, 2 * owner + 1 - at.pair_at
            if route == "A":
                for_pair = part(pair_block, piece).astype(bf16)
                total = part(own_block, piece)
                total = total + at.pair(for_pair).astype(f32)
            else:
                total = jnp.stack([part(own_block, piece), part(pair_block, piece)])
            if carried is not None:
                total = total + carried.astype(f32)
            if step + 1 < at.ring_size:
                carried = at.ring(total.astype(bf16))
        if route == "B":
            total = total[0] + at.pair(total[1].astype(bf16)).astype(f32)
        totals.append(total)
    return jnp.concatenate(totals, axis=1)


def half_of(value, which):
    size = value.shape[0] // 2
    return lax.dynamic_slice_in_dim(value, which * size, size, axis=0)


def summed_half(at, partial):
    for_other = half_of(partial, 1 - at.core)
    mine = half_of(partial, at.core).astype(f32)
    chip = mine + at.other_core(for_other).astype(f32)
    return at.chips_sum(chip.astype(bf16))


def both_halves(at, half):
    other = at.other_core(half)
    first = jnp.where(at.core == 0, half, other)
    second = jnp.where(at.core == 0, other, half)
    return jnp.concatenate([first, second], axis=0)


def normalize(values):
    center = jnp.mean(values, axis=-1, keepdims=True)
    offset = values - center
    spread = jnp.mean(offset * offset, axis=-1, keepdims=True)
    scale = lax.rsqrt(spread + norm_epsilon)
    return offset * scale, scale


def norm_back(grad, normal, scale, gain):
    gain_grad = jnp.sum(grad * normal, axis=0)
    shift_grad = jnp.sum(grad, axis=0)
    e = grad * gain
    mean_e = jnp.mean(e, axis=-1, keepdims=True)
    mean_en = jnp.mean(e * normal, axis=-1, keepdims=True)
    return scale * (e - mean_e - normal * mean_en), gain_grad, shift_grad


def gelu_exact(values):
    below = 0.5 * (1.0 + lax.erf(values * 0.5**0.5))
    density = jnp.exp(-0.5 * values * values) * (2.0 * jnp.pi) ** -0.5
    return values * below, below + values * density


def row_weights(item_lengths, item_actions, slot_count):
    position = jnp.arange(slot_count, dtype=jnp.int32)
    in_step = position % STEP_SLOTS
    counts = jnp.repeat(item_actions, STEP_SLOTS, axis=1)
    is_valid = position[None, :] < item_lengths[:, None]
    is_action = in_step[None, :] >= STEP_SLOTS - counts
    return jnp.where(is_valid, jnp.where(is_action, 1.0, 0.5), 0.0).astype(f32)


def causal_allowed(item_lengths, slot_count):
    position = jnp.arange(slot_count, dtype=jnp.int32)
    return (position[None, None, :] <= position[None, :, None]) & (
        position[None, None, :] < item_lengths[:, None, None]
    )


def masked_scores(queries, key_heads, allowed):
    scores = dot("cqhd,ckhd->chqk", queries, key_heads) * HEAD_DIM ** (-0.5)
    return jnp.where(allowed[:, None], scores, masked_score)


def layer(
    tokens,
    cotangent,
    lengths,
    action_counts,
    qkv_weight,
    out_weight,
    up_weight,
    down_weight,
    gain_one,
    shift_one,
    gain_two,
    shift_two,
):
    at = Places()
    item_count, slot_count, width = tokens.shape
    rows = item_count * slot_count
    shard_rows, kinds, head_width = qkv_weight.shape

    norm_params = jnp.stack([gain_one, shift_one, gain_two, shift_two])
    norm_params = gather(at, norm_params)
    norm_params = norm_params.reshape(at.dp, 4, shard_rows).transpose(1, 0, 2)
    gain_1, shift_1, gain_2, shift_2 = norm_params.reshape(4, width).astype(f32)
    qkv_w = gather(at, qkv_weight.reshape(shard_rows, kinds * head_width))
    out_w = gather(at, out_weight)
    up_w = gather(at, up_weight)
    down_w = gather(at, down_weight)

    tokens_f = tokens.astype(f32).reshape(rows, width)
    weighting = row_weights(lengths, action_counts, slot_count).reshape(rows, 1)
    grad_out = cotangent.astype(f32).reshape(rows, width) * weighting
    grad_low = grad_out.astype(bf16)

    normal_1, _ = normalize(tokens_f)
    normed_one = (normal_1 * gain_1 + shift_1).astype(bf16)
    projected = dot("rd,df->rf", normed_one, qkv_w).astype(bf16)
    projected = projected.reshape(rows, kinds, head_width)
    head_shape = (item_count, slot_count, head_width // HEAD_DIM, HEAD_DIM)
    queries = projected[:, 0].reshape(head_shape)
    key_heads = projected[:, 1].reshape(head_shape)
    value_heads = projected[:, 2].reshape(head_shape)
    allowed = causal_allowed(lengths, slot_count)
    scores = masked_scores(queries, key_heads, allowed)
    row_max = jnp.max(scores, axis=-1, keepdims=True)
    exponent = jnp.exp(scores - row_max)
    row_total = jnp.sum(exponent, axis=-1, keepdims=True)
    log_total = row_max + jnp.log(row_total)
    probs_low = (exponent / row_total).astype(bf16)
    attended = dot("chqk,ckhd->cqhd", probs_low, value_heads).astype(bf16)
    attended = attended.reshape(rows, head_width)

    branch = summed_half(at, dot("rh,dh->rd", attended, out_w).astype(bf16))
    tokens_half = half_of(tokens_f, at.core)
    middle = tokens_half + branch
    normal_2, scale_2 = normalize(middle)
    normed_two = both_halves(at, (normal_2 * gain_2 + shift_2).astype(bf16))

    up_proj = dot("rd,df->rf", normed_two, up_w)
    activated, slope = gelu_exact(up_proj)
    activated = activated.astype(bf16)
    down_grad = weight_grad(at, grad_low, activated)
    grad_act = dot("rd,df->rf", grad_low, down_w)
    grad_up = (grad_act * slope).astype(bf16)

    grad_normed_two = summed_half(at, dot("rf,df->rd", grad_up, up_w).astype(bf16))
    down_proj = summed_half(at, dot("rf,df->rd", activated, down_w).astype(bf16))
    layer_out = both_halves(at, (middle + down_proj).astype(bf16))
    up_grad = weight_grad(at, normed_two, grad_up)

    grad_middle, gain_two_grad, shift_two_grad = norm_back(
        grad_normed_two, normal_2, scale_2, gain_2
    )
    grad_middle = grad_middle + half_of(grad_out, at.core)
    grad_branch = both_halves(at, grad_middle.astype(bf16))
    out_grad = weight_grad(at, grad_branch, attended)
    grad_attended = dot("rd,dh->rh", grad_branch, out_w).astype(bf16).reshape(head_shape)

    exact_probs = jnp.exp(masked_scores(queries, key_heads, allowed) - log_total)
    grad_value = dot("chqk,cqhd->ckhd", exact_probs.astype(bf16), grad_attended).astype(bf16)
    grad_probs = dot("cqhd,ckhd->chqk", grad_attended, value_heads)
    inner = jnp.sum(exact_probs * grad_probs, axis=-1, keepdims=True)
    grad_scores = (exact_probs * (grad_probs - inner)).astype(bf16)
    scaling = HEAD_DIM ** (-0.5)
    grad_query = (dot("chqk,ckhd->cqhd", grad_scores, key_heads) * scaling).astype(bf16)
    grad_key = (dot("chqk,cqhd->ckhd", grad_scores, queries) * scaling).astype(bf16)
    grad_projected = jnp.concatenate(
        [part.reshape(rows, head_width) for part in (grad_query, grad_key, grad_value)], axis=1
    )

    grad_normed_one = summed_half(at, dot("rf,df->rd", grad_projected, qkv_w).astype(bf16))
    qkv_grad = weight_grad(at, normed_one, grad_projected)
    normal_half, scale_half = normalize(tokens_half)
    grad_tokens, gain_one_grad, shift_one_grad = norm_back(
        grad_normed_one, normal_half, scale_half, gain_1
    )
    input_grad = both_halves(at, grad_tokens + grad_middle)

    norm_grads = jnp.stack([gain_one_grad, shift_one_grad, gain_two_grad, shift_two_grad])
    norm_grads = norm_grads + at.other_core(norm_grads)
    blocks = norm_grads.reshape(4, at.dp, shard_rows).transpose(1, 0, 2)
    norm_total = lax.dynamic_index_in_dim(blocks, at.dp_at, axis=0, keepdims=False)
    for by in range(1, at.dp):
        block = lax.dynamic_index_in_dim(
            blocks, (at.dp_at + by) % at.dp, axis=0, keepdims=False
        )
        norm_total = norm_total + at.shift(block, by)

    return (
        layer_out.reshape(tokens.shape),
        input_grad.reshape(tokens.shape),
        qkv_grad.reshape(qkv_weight.shape),
        out_grad,
        up_grad,
        down_grad,
        norm_total[0],
        norm_total[1],
        norm_total[2],
        norm_total[3],
    )


def solution(mesh):
    return step_of(mesh)


def step_of(mesh):
    weight = P("dp", "tp")
    return jax.shard_map(
        layer,
        mesh=mesh,
        in_specs=(
            P("dp", None, None),
            P("dp", None, None),
            P("dp"),
            P("dp", None),
            P("dp", None, "tp"),
            weight,
            weight,
            weight,
            P("dp"),
            P("dp"),
            P("dp"),
            P("dp"),
        ),
        out_specs=(
            P("dp", None, None),
            P("dp", None, None),
            P("dp", None, "tp"),
            weight,
            weight,
            weight,
            P("dp"),
            P("dp"),
            P("dp"),
            P("dp"),
        ),
        check_vma=False,
    )
```
